32 devices in a mesh: gx: 4 (over z), gy: 4 (over y, core), gz: 2 (over x).
Axes of the slice: x: 2, y: 2, z: 4, core: 2. Of those that a mesh axis runs over, the one named last changes fastest.
Arguments:
- grads: float32 [4, 4, 2, 16, 14336], P('gx', 'gy', 'gz'), may hold values from -100 to 100
- plan: int32 [3], replicated, may hold values from 0 to 2, each once
Outputs:
- averaged: float32 [4, 4, 2, 16, 14336], P('gx', 'gy', 'gz')
- reports: float32 [3], replicated
The draws below stay inside these ranges and needn't reach their ends.
Inputs may be any that keep to these rules, and one draw needn't show every extreme that they name: `plan`: each of 0, 1, 2 appears once.
All inputs are finite; a program needn't handle non-finite values.
Results may differ from the reference program's by a relative error of at most 0.0003.
Values sent between devices are 32-bit elements; how exact they have to be, the bound alone decides.
A program may use at most 64 MiB of HBM per device.

```python
import math
import jax
import jax.numpy as jnp
from jax import lax

FF = 14336
ROWS = 16
N_GX = 4
N_GY = 4
N_GZ = 2


def draw_grads(key, part):
    first, second = jax.random.split(jax.random.fold_in(key, 17), 2)
    scales = jnp.exp(jax.random.uniform(first, (N_GX, N_GY, N_GZ, 1, 1), jnp.float32) * math.log(3.0))
    base = jax.random.normal(second, (N_GX, N_GY, N_GZ, ROWS, FF), jnp.float32)
    base = jnp.clip(base, -6.0, 6.0)
    return (base * scales).astype(jnp.float32)


def setup_inputs(seed: int = 0) -> dict:
    key_of = jax.random.split(jax.random.key(seed), 3)
    return {
        "grads": draw_grads(jax.random.fold_in(key_of[2], 71), 0),
        "plan": jax.random.permutation(key_of[1], 3).astype(jnp.int32),
    }


def one_round(current, axis_id):
    def along(dim):
        def inner(value):
            total = jnp.sum(value, axis=dim, keepdims=True)
            return jnp.broadcast_to(total / value.shape[dim], value.shape)
        return inner
    group = lax.switch(axis_id, [along(0), along(1), along(2)], current)
    deviation = jnp.max(jnp.abs(current - group))
    return group, deviation


def reference(grads, plan):
    current = grads
    values = []
    for step in range(3):
        current, deviation = one_round(current, plan[step])
        values.append(deviation)
    return current, jnp.stack(values).astype(jnp.float32)
```

```python
import functools
import math

import jax
import jax.numpy as jnp
from jax import lax
from jax.experimental import pallas as pl
from jax.experimental.pallas import tpu as pltpu
from jax.sharding import PartitionSpec as P

AXES = ("gx", "gy", "gz")
LANES = 128
SUBLANES = 8
CHUNKS = 3
STEP_US = 2.0
FIRST_US = (20.0, 10.0, 10.0)


def power_of_two(n):
    return n & (n - 1) == 0


def mean_of(total, n):
    return total * (1.0 / n) if power_of_two(n) else total / n


def chunks_of(p):
    count = min(CHUNKS, p)
    bounds = [p * k // count for k in range(count + 1)]
    return [(lo, hi - lo) for lo, hi in zip(bounds[:-1], bounds[1:])]


def gather_stages(sizes, turn):
    bits = []
    if power_of_two(sizes[1]):
        bit = sizes[1] // 2
        while bit:
            bits.append((1, bit))
            bit //= 2
        head, tail = bits[:-1], bits[-1:]
    else:
        head, tail = [(1, None)], []
    middle = [(2, None)] + head if turn % 2 == 0 else head + [(2, None)]
    return [(0, None)] + middle + tail


class Copies:
    def __init__(self, send, recv):
        self.send, self.recv, self.count, self.all = send, recv, 0, []

    def start(self, src, dst, axis, peer):
        copy = pltpu.make_async_remote_copy(
            src_ref=src,
            dst_ref=dst,
            send_sem=self.send.at[self.count],
            recv_sem=self.recv.at[self.count],
            device_id={AXES[axis]: peer},
            device_id_type=pl.DeviceIdType.MESH,
        )
        self.count += 1
        copy.start()
        self.all.append(copy)
        return copy


def kernel(order, sizes, p, x, out, reports, own, recv0, recv1, recv2, cur0, cur1, dev, rep, rep_recv, send_sem, recv_sem, own_sem):
    me = [lax.axis_index(name) for name in AXES]
    parts = chunks_of(p)
    recvs = (recv0, recv1, recv2)
    curs = (own, cur0, cur1)

    barrier = pltpu.get_barrier_semaphore()
    peers = 0
    for axis in range(3):
        for d in range(1, sizes[axis]):
            peer = lax.rem(me[axis] + d, sizes[axis])
            pl.semaphore_signal(barrier, inc=1, device_id={AXES[axis]: peer}, device_id_type=pl.DeviceIdType.MESH)
            peers += 1

    owns = []
    for k, (lo, size) in enumerate(parts):
        index = [slice(None)] * 3
        index[order[0]] = me[order[0]]
        copy = pltpu.make_async_copy(
            x.at[(*index, pl.ds(lo, size))], own.at[(slice(None), slice(None), pl.ds(lo, size))], own_sem.at[k]
        )
        copy.start()
        owns.append(copy)
    dev[...] = jnp.zeros_like(dev)
    pl.semaphore_wait(barrier, peers)

    copies = Copies(send_sem, recv_sem)
    waiting = {}

    def scatter(r, k):
        axis = order[r]
        n = sizes[axis]
        lo, size = parts[k]
        left = sorted(order[r:])
        source = x if r == 0 else curs[r]
        started = []
        for d in range(1, n):
            peer = lax.rem(me[axis] + d, n)
            index = tuple(peer if a == axis else slice(None) for a in left)
            rest = (slice(None),) * (len(left) - 1)
            started.append(
                copies.start(
                    source.at[(*index, pl.ds(lo, size))], recvs[r].at[(d - 1, *rest, pl.ds(lo, size))], axis, peer
                )
            )
        waiting[r, k] = started

    def settle(r, k):
        axis = order[r]
        n = sizes[axis]
        lo, size = parts[k]
        for copy in waiting[r, k]:
            copy.wait_recv()
        if r == 0:
            owns[k].wait()
        rest = sorted(order[r + 1 :])
        span = pl.ds(lo, size)
        worst = None
        places = [()]
        for a in rest:
            places = [place + (i,) for place in places for i in range(sizes[a])]
        for place in places:
            if r == 0:
                mine = own[(*place, span)]
            else:
                full = list(place)
                full.insert(sorted(order[r:]).index(axis), me[axis])
                mine = curs[r][(*full, span)]
            values = [mine] + [recvs[r][(d, *place, span)] for d in range(n - 1)]
            group = mean_of(functools.reduce(jnp.add, values), n)
            for value in values:
                gap = jnp.max(jnp.abs(value - group), axis=0)
                worst = gap if worst is None else jnp.maximum(worst, gap)
            if r == 2:
                out[(me[0], me[1], me[2], span)] = group
            else:
                curs[r + 1][(*place, span)] = group
        dev[r] = jnp.maximum(dev[r], worst)

    held = {}

    def gather(k, stage):
        axis, bit = gather_stages(sizes, k)[stage]
        n = sizes[axis]
        span = pl.ds(*parts[k])
        if stage == 0:
            held[k] = [[me[0]], [me[1]], [me[2]]]
        have = held[k]
        blocks = [[]]
        for a in range(3):
            choices = [slice(None)] if have[a] is None else have[a]
            blocks = [block + [c] for block in blocks for c in choices]
        if bit is None:
            partners = [lax.rem(me[axis] + d, n) for d in range(1, n)]
        else:
            high = lax.rem(me[axis] // bit, 2)
            partners = [me[axis] + bit - 2 * bit * high]
        started = []
        for peer in partners:
            for block in blocks:
                piece = out.at[(*block, span)]
                started.append(copies.start(piece, piece, axis, peer))
        waiting["gather", k] = started
        if bit is None or bit == 1:
            have[axis] = None
        else:
            high = lax.rem(me[axis] // bit, 2)
            have[axis] = have[axis] + [i + bit - 2 * bit * high for i in have[axis]]

    def landed(k):
        for copy in waiting["gather", k]:
            copy.wait_recv()

    def tell(axis):
        slot = sum(sizes[a] - 1 for a in range(axis))
        if axis == 0:
            rows = lax.broadcasted_iota(jnp.int32, (SUBLANES, LANES), 0)
            tile = jnp.zeros((SUBLANES, LANES), jnp.float32)
            for r in range(3):
                tile = jnp.where(rows == r, jnp.max(dev[r]), tile)
            rep[0] = tile
        started = []
        for d in range(1, sizes[axis]):
            peer = lax.rem(me[axis] + d, sizes[axis])
            started.append(copies.start(rep.at[axis], rep_recv.at[slot + d - 1], axis, peer))
        waiting["rep", axis] = started

    def told(axis):
        slot = sum(sizes[a] - 1 for a in range(axis))
        for copy in waiting["rep", axis]:
            copy.wait_recv()
        tile = rep[axis]
        for d in range(1, sizes[axis]):
            tile = jnp.maximum(tile, rep_recv[slot + d - 1])
        if axis < 2:
            rep[axis + 1] = tile
        else:
            for r in range(3):
                reports[r] = jnp.max(tile[r : r + 1])

    for k in range(len(parts)):
        scatter(0, k)

    events = []
    for k in range(len(parts)):
        at = FIRST_US[order[0]] * (k + 1) / len(parts)

        def reduce_step(k=k, r=0):
            settle(r, k)
            if r < 2:
                scatter(r + 1, k)
            else:
                gather(k, 0)

        for r in range(3):
            events.append((at + r * STEP_US, k, functools.partial(reduce_step, k, r)))
        last = len(gather_stages(sizes, k))
        for stage in range(1, last + 1):

            def gather_step(k=k, stage=stage, last=last):
                landed(k)
                if stage < last:
                    gather(k, stage)

            events.append((at + (2 + stage) * STEP_US, k, functools.partial(gather_step, k, stage, last)))
        if k == len(parts) - 1:
            events.append((at + 2 * STEP_US + 0.1, k, lambda: tell(0)))
            for axis in range(3):

                def rep_step(axis=axis):
                    told(axis)
                    if axis < 2:
                        tell(axis + 1)

                events.append((at + (3 + axis) * STEP_US + 0.1, k, functools.partial(rep_step, axis)))
    for _, _, step in sorted(events, key=lambda event: event[:2]):
        step()
    for copy in copies.all:
        copy.wait_send()


def copy_count(sizes, p):
    lines = sum(n - 1 for n in sizes)
    total = lines
    for k in range(len(chunks_of(p))):
        total += lines
        pieces = 1
        for axis, bit in gather_stages(sizes, k):
            if bit is None:
                total += (sizes[axis] - 1) * pieces
                pieces = pieces if axis != 1 else 1
            else:
                total += pieces
                pieces = 1 if bit == 1 else pieces * 2
    return total


def run(which, order, sizes, p, x):
    tile = (SUBLANES, LANES)
    copies = copy_count(sizes, p)
    rest = [tuple(sizes[a] for a in sorted(order[r + 1 :])) for r in range(3)]
    f32 = jnp.float32
    scratch = [pltpu.VMEM((*rest[0], p, *tile), f32)]
    scratch += [pltpu.VMEM((sizes[order[r]] - 1, *rest[r], p, *tile), f32) for r in range(3)]
    scratch += [pltpu.VMEM((*rest[r], p, *tile), f32) for r in range(2)]
    scratch += [
        pltpu.VMEM((3, *tile), f32),
        pltpu.VMEM((3, *tile), f32),
        pltpu.VMEM((sum(n - 1 for n in sizes), *tile), f32),
        pltpu.SemaphoreType.DMA((copies,)),
        pltpu.SemaphoreType.DMA((copies,)),
        pltpu.SemaphoreType.DMA((len(chunks_of(p)),)),
    ]
    return pl.pallas_call(
        functools.partial(kernel, order, sizes, p),
        out_shape=(jax.ShapeDtypeStruct(x.shape, f32), jax.ShapeDtypeStruct((3,), f32)),
        in_specs=[pl.BlockSpec(memory_space=pl.ANY)],
        out_specs=(pl.BlockSpec(memory_space=pltpu.VMEM), pl.BlockSpec(memory_space=pltpu.SMEM)),
        scratch_shapes=scratch,
        compiler_params=pltpu.CompilerParams(collective_id=which, has_side_effects=True),
        name=f"moshpit_{which}",
    )(x)


def on_device(sizes, grads, plan):
    rows, columns = grads.shape[-2:]
    high, wide = rows // SUBLANES, columns // LANES
    tiles = high * wide
    p = -(-tiles // math.prod(sizes))
    x = grads.reshape(high, SUBLANES, wide, LANES).transpose(0, 2, 1, 3).reshape(tiles, SUBLANES, LANES)
    spare = p * math.prod(sizes) - tiles
    if spare:
        x = jnp.pad(x, ((0, spare), (0, 0), (0, 0)))
    x = x.reshape(*sizes, p, SUBLANES, LANES)
    orders = [(a, b, 3 - a - b) for a in range(3) for b in range(3) if a != b]
    branches = [functools.partial(run, i, order, sizes, p) for i, order in enumerate(orders)]
    choice = 2 * plan[0] + (plan[1] > plan[2]).astype(jnp.int32)
    out, reports = lax.switch(choice, branches, x)
    out = out.reshape(-1, SUBLANES, LANES)[:tiles]
    out = out.reshape(high, wide, SUBLANES, LANES).transpose(0, 2, 1, 3).reshape(grads.shape)
    return out, reports


def solution(mesh):
    sizes = tuple(mesh.shape[name] for name in AXES)
    placed = (P("gx", "gy", "gz", None, None), P())
    return jax.shard_map(
        functools.partial(on_device, sizes), mesh=mesh, in_specs=placed, out_specs=placed, check_vma=False
    )
```

```python
import functools
import itertools
import math

import jax
import jax.numpy as jnp
from jax import lax
from jax.experimental import pallas as pl
from jax.experimental.pallas import tpu as pltpu
from jax.sharding import PartitionSpec as P

AXES = ("gx", "gy", "gz")
LANES = 128
SUBLANES = 8
PLANS = {
    (0, 1, 2): (((0, 1, 2),), (3, 3, 1)),
    (0, 2, 1): (((0, 2, 1),), (3, 3, 1)),
    (1, 0, 2): (((1,), (0, 2)), (3, 2, 1, 1)),
    (1, 2, 0): (((1, 2), (0,)), (3, 2, 1, 1)),
    (2, 0, 1): (((2,), (0, 1)), (3, 2, 1, 1)),
    (2, 1, 0): (((2, 1), (0,)), (3, 2, 1, 1)),
}
FIRST_US = (20.0, 10.0, 10.0)
STEP_US = 3.0


def power_of_two(n):
    return n & (n - 1) == 0


def mean_of(total, n):
    return total * (1.0 / n) if power_of_two(n) else total / n


def chunks_of(p, shares):
    total, bounds, done = sum(shares), [0], 0
    for share in shares:
        done += share
        bounds.append(p * done // total)
    return [(lo, hi - lo) for lo, hi in zip(bounds[:-1], bounds[1:]) if hi > lo]


def gather_stages(sizes):
    if not power_of_two(sizes[1]):
        return [[(0, None)], [(2, None)], [(1, None)]]
    bits, bit = [], sizes[1] // 2
    while bit:
        bits.append((1, bit))
        bit //= 2
    return [[(0, None)], [(2, None)] + bits[:-1], bits[-1:]]


def gather_count(sizes):
    total, held = 0, [1, 1, 1]
    for stage in gather_stages(sizes):
        total += math.prod(held) * (math.prod(sizes[a] if bit is None else 2 for a, bit in stage) - 1)
        for axis, bit in stage:
            held[axis] = 1 if bit is None or bit == 1 else 2 * held[axis]
    return total


def offsets_of(axes, sizes):
    found = itertools.product(*[range(sizes[a]) if a in axes else (0,) for a in range(3)])
    return [d for d in sorted(found, key=lambda d: sum(min(i, n - i) for i, n in zip(d, sizes))) if any(d)]


class Copies:
    def __init__(self, send, recv):
        self.send, self.recv, self.count, self.all = send, recv, 0, []

    def start(self, src, dst, peer):
        copy = pltpu.make_async_remote_copy(
            src_ref=src,
            dst_ref=dst,
            send_sem=self.send.at[self.count],
            recv_sem=self.recv.at[self.count],
            device_id=tuple(peer),
            device_id_type=pl.DeviceIdType.MESH,
        )
        self.count += 1
        copy.start()
        self.all.append(copy)
        return copy


def kernel(order, sizes, p, x, out, reports, own, dev, rep, rep_recv, send_sem, recv_sem, own_sem, *bufs):
    groups, shares = PLANS[order]
    me = [lax.axis_index(name) for name in AXES]
    parts = chunks_of(p, shares)
    recvs = bufs[: len(groups)]
    curs = (own,) + bufs[len(groups) :]
    stages = gather_stages(sizes)
    rep_groups = ((0,), (1, 2))

    def peer_at(d):
        return [lax.rem(me[a] + d[a], sizes[a]) if d[a] else me[a] for a in range(3)]

    barrier = pltpu.get_barrier_semaphore()
    near = [set(group) for group in groups] + [set(group) for group in rep_groups]
    near += [{axis for axis, _ in stage} for stage in stages]
    greeted = [d for d in offsets_of((0, 1, 2), sizes) if any({a for a in range(3) if d[a]} <= axes for axes in near)]
    for d in greeted:
        pl.semaphore_signal(barrier, inc=1, device_id=tuple(peer_at(d)), device_id_type=pl.DeviceIdType.MESH)

    owns = []
    for k, (lo, size) in enumerate(parts):
        index = [me[a] if a in groups[0] else slice(None) for a in range(3)]
        rest = (slice(None),) * (3 - len(groups[0]))
        copy = pltpu.make_async_copy(x.at[(*index, pl.ds(lo, size))], own.at[(*rest, pl.ds(lo, size))], own_sem.at[k])
        copy.start()
        owns.append(copy)
    dev[...] = jnp.zeros_like(dev)
    pl.semaphore_wait(barrier, len(greeted))

    copies = Copies(send_sem, recv_sem)
    waiting = {}

    def left_at(g):
        return sorted(a for group in groups[g:] for a in group)

    def scatter(g, k):
        span = pl.ds(*parts[k])
        source = x if g == 0 else curs[g]
        left, rest = left_at(g), left_at(g + 1)
        waiting[g, k] = []
        for slot, d in enumerate(offsets_of(groups[g], sizes)):
            peer = peer_at(d)
            index = tuple(peer[a] if a in groups[g] else slice(None) for a in left)
            place = recvs[g].at[(slot, *[slice(None)] * len(rest), span)]
            waiting[g, k].append(copies.start(source.at[(*index, span)], place, peer))

    def settle(g, k):
        for copy in waiting[g, k]:
            copy.wait_recv()
        if g == 0:
            owns[k].wait()
        lo, size = parts[k]
        left, rest = left_at(g), left_at(g + 1)
        first = sum(len(group) for group in groups[:g])
        worst = {}
        for place in itertools.product(*[range(sizes[a]) for a in rest]):
            for t in range(lo, lo + size):
                where = dict(zip(rest, place))
                if g == 0:
                    mine = own[(*place, t)]
                else:
                    mine = curs[g][(*[where.get(a, me[a]) for a in left], t)]
                values = {(0, 0, 0): mine}
                for slot, d in enumerate(offsets_of(groups[g], sizes)):
                    values[d] = recvs[g][(slot, *place, t)]
                for r, axis in enumerate(groups[g], first):
                    members = {}
                    for d, value in values.items():
                        members.setdefault((*d[:axis], 0, *d[axis + 1 :]), []).append(value)
                    values = {}
                    for d, group in members.items():
                        mean = mean_of(functools.reduce(jnp.add, group), len(group))
                        values[d] = mean
                        for value in group:
                            gap = jnp.abs(value - mean)
                            worst[r] = jnp.maximum(worst[r], gap) if r in worst else gap
                (mean,) = values.values()
                if g == len(groups) - 1:
                    out[(me[0], me[1], me[2], t)] = mean
                else:
                    curs[g + 1][(*place, t)] = mean
        for r, gap in worst.items():
            dev[r] = jnp.maximum(dev[r], gap)

    held = {}

    def gather(k, s):
        span = pl.ds(*parts[k])
        if s == 0:
            held[k] = [[me[0]], [me[1]], [me[2]]]
        have = held[k]
        blocks = list(itertools.product(*[[slice(None)] if h is None else h for h in have]))
        choices = []
        for axis, bit in stages[s]:
            if bit is None:
                n = sizes[axis]
                choices.append([(axis, me[axis])] + [(axis, lax.rem(me[axis] + d, n)) for d in range(1, n)])
            else:
                choices.append([(axis, bit, 0), (axis, bit, 1)])
        waiting["gather", k] = []
        for number, choice in enumerate(itertools.product(*choices)):
            if number == 0:
                continue
            peer = list(me)
            flips = 0
            for part in choice:
                if len(part) == 2:
                    peer[part[0]] = part[1]
                elif part[2]:
                    high = lax.rem(me[part[0]] // part[1], 2)
                    flips = flips + part[1] - 2 * part[1] * high
                    peer[part[0]] = me[part[0]] + flips
            for block in blocks:
                piece = out.at[(*block, span)]
                waiting["gather", k].append(copies.start(piece, piece, peer))
        for axis, bit in stages[s]:
            if bit is None or bit == 1:
                have[axis] = None
            else:
                turn = bit - 2 * bit * lax.rem(me[axis] // bit, 2)
                have[axis] = have[axis] + [i + turn for i in have[axis]]

    def landed(k):
        for copy in waiting["gather", k]:
            copy.wait_recv()

    def tell(s):
        base = sum(len(offsets_of(group, sizes)) for group in rep_groups[:s])
        if s == 0:
            rows = lax.broadcasted_iota(jnp.int32, (SUBLANES, LANES), 0)
            tile = jnp.zeros((SUBLANES, LANES), jnp.float32)
            for r in range(3):
                tile = jnp.where(rows == r, jnp.max(dev[r]), tile)
            rep[0] = tile
        waiting["rep", s] = []
        for slot, d in enumerate(offsets_of(rep_groups[s], sizes), base):
            waiting["rep", s].append(copies.start(rep.at[s], rep_recv.at[slot], peer_at(d)))

    def told(s):
        base = sum(len(offsets_of(group, sizes)) for group in rep_groups[:s])
        for copy in waiting["rep", s]:
            copy.wait_recv()
        tile = rep[s]
        for slot in range(base, base + len(waiting["rep", s])):
            tile = jnp.maximum(tile, rep_recv[slot])
        if s == 0:
            rep[1] = tile
        else:
            for r in range(3):
                reports[r] = jnp.max(tile[r : r + 1])

    for k in range(len(parts)):
        scatter(0, k)

    events = []
    whole = FIRST_US[order[0]]
    for k, (lo, size) in enumerate(parts):
        at = whole * (lo + size) / p

        def reduce_step(g, k):
            settle(g, k)
            if g + 1 < len(groups):
                scatter(g + 1, k)
            else:
                gather(k, 0)

        for g in range(len(groups)):
            events.append((at + g * STEP_US, k, functools.partial(reduce_step, g, k)))
        if order[0] == 0:
            at = whole
        at += (len(groups) - 1) * STEP_US

        def gather_step(k, s):
            landed(k)
            if s < len(stages):
                gather(k, s)

        for s in range(1, len(stages) + 1):
            events.append((at + s * STEP_US, k, functools.partial(gather_step, k, s)))
        if k == len(parts) - 1:

            def rep_step(s):
                if s:
                    told(s - 1)
                if s < 2:
                    tell(s)

            for s in range(3):
                events.append((at + s * STEP_US + 0.1, k, functools.partial(rep_step, s)))
    for _, _, step in sorted(events, key=lambda event: event[:2]):
        step()
    for copy in copies.all:
        copy.wait_send()


def run(which, order, sizes, p, x):
    tile = (SUBLANES, LANES)
    f32 = jnp.float32
    groups, shares = PLANS[order]
    parts = len(chunks_of(p, shares))
    reps = len(offsets_of((0,), sizes)) + len(offsets_of((1, 2), sizes))
    copies = reps + parts * sum(len(offsets_of(group, sizes)) for group in groups)
    copies += parts * gather_count(sizes)
    recvs, curs = [], []
    for g, group in enumerate(groups):
        rest = [sizes[a] for a in sorted(a for later in groups[g + 1 :] for a in later)]
        recvs.append(pltpu.VMEM((len(offsets_of(group, sizes)), *rest, p, *tile), f32))
        if g == 0:
            own = pltpu.VMEM((*rest, p, *tile), f32)
        if g + 1 < len(groups):
            curs.append(pltpu.VMEM((*rest, p, *tile), f32))
    scratch = [own, pltpu.VMEM((3, *tile), f32), pltpu.VMEM((2, *tile), f32), pltpu.VMEM((reps, *tile), f32)]
    scratch += [pltpu.SemaphoreType.DMA((copies,)), pltpu.SemaphoreType.DMA((copies,)), pltpu.SemaphoreType.DMA((parts,))]
    return pl.pallas_call(
        functools.partial(kernel, order, sizes, p),
        out_shape=(jax.ShapeDtypeStruct(x.shape, f32), jax.ShapeDtypeStruct((3,), f32)),
        in_specs=[pl.BlockSpec(memory_space=pl.ANY)],
        out_specs=(pl.BlockSpec(memory_space=pltpu.VMEM), pl.BlockSpec(memory_space=pltpu.SMEM)),
        scratch_shapes=scratch + recvs + curs,
        compiler_params=pltpu.CompilerParams(collective_id=which, has_side_effects=True),
        name=f"moshpit_{which}",
    )(x)


def on_device(sizes, grads, plan):
    rows, columns = grads.shape[-2:]
    high, wide = rows // SUBLANES, columns // LANES
    tiles = high * wide
    p = -(-tiles // math.prod(sizes))
    x = grads.reshape(high, SUBLANES, wide, LANES).transpose(0, 2, 1, 3).reshape(tiles, SUBLANES, LANES)
    spare = p * math.prod(sizes) - tiles
    if spare:
        x = jnp.pad(x, ((0, spare), (0, 0), (0, 0)))
    x = x.reshape(*sizes, p, SUBLANES, LANES)
    orders = [(0, 1, 2), (0, 2, 1), (1, 0, 2), (1, 2, 0), (1, 2, 0), (2, 0, 1), (2, 1, 0)]
    names = {order: i for i, order in enumerate(PLANS)}
    branches = [functools.partial(run, names[order], order, sizes, p) for order in orders]
    place = lax.iota(jnp.int32, 3)
    choice = jnp.sum(plan * ((3 - place) * (2 - place) // 2)) - 1
    out, reports = lax.switch(choice, branches, x)
    out = out.reshape(-1, SUBLANES, LANES)[:tiles]
    out = out.reshape(high, wide, SUBLANES, LANES).transpose(0, 2, 1, 3).reshape(grads.shape)
    return out, reports


def solution(mesh):
    sizes = tuple(mesh.shape[name] for name in AXES)
    placed = (P("gx", "gy", "gz", None, None), P())
    return jax.shard_map(
        functools.partial(on_device, sizes), mesh=mesh, in_specs=placed, out_specs=placed, check_vma=False
    )
```

```python
import functools
import itertools
import math

import jax
import jax.numpy as jnp
from jax import lax
from jax.experimental import pallas as pl
from jax.experimental.pallas import tpu as pltpu
from jax.sharding import PartitionSpec as P

AXES = ("gx", "gy", "gz")
LANES = 128
SUBLANES = 8
PLANS = {
    (0, 1, 2): (((0, 1, 2),), (3, 3, 1)),
    (0, 2, 1): (((0, 2, 1),), (3, 3, 1)),
    (1, 0, 2): (((1,), (0, 2)), (3, 2, 1, 1)),
    (1, 2, 0): (((1, 2), (0,)), (3, 2, 1, 1)),
    (2, 0, 1): (((2,), (0, 1)), (2, 2, 2, 1)),
    (2, 1, 0): (((2, 1), (0,)), (3, 2, 1, 1)),
}
FIRST_US = (20.0, 10.0, 10.0)
STEP_US = 3.0


def power_of_two(n):
    return n & (n - 1) == 0


def mean_of(total, n):
    return total * (1.0 / n) if power_of_two(n) else total / n


def chunks_of(p, shares):
    total, bounds, done = sum(shares), [0], 0
    for share in shares:
        done += share
        bounds.append(p * done // total)
    return [(lo, hi - lo) for lo, hi in zip(bounds[:-1], bounds[1:]) if hi > lo]


def gather_stages(sizes):
    if not power_of_two(sizes[1]):
        return [[(0, None)], [(2, None)], [(1, None)]]
    bits, bit = [], sizes[1] // 2
    while bit:
        bits.append((1, bit))
        bit //= 2
    return [[(0, None)], [(2, None)] + bits[:-1], bits[-1:]]


def gather_count(sizes):
    total, held = 0, [1, 1, 1]
    for stage in gather_stages(sizes):
        total += math.prod(held) * (math.prod(sizes[a] if bit is None else 2 for a, bit in stage) - 1)
        for axis, bit in stage:
            held[axis] = 1 if bit is None or bit == 1 else 2 * held[axis]
    return total


def offsets_of(axes, sizes):
    found = itertools.product(*[range(sizes[a]) if a in axes else (0,) for a in range(3)])
    return [d for d in sorted(found, key=lambda d: sum(min(i, n - i) for i, n in zip(d, sizes))) if any(d)]


class Copies:
    def __init__(self, send, recv):
        self.send, self.recv, self.count, self.all = send, recv, 0, []

    def start(self, src, dst, peer):
        copy = pltpu.make_async_remote_copy(
            src_ref=src,
            dst_ref=dst,
            send_sem=self.send.at[self.count],
            recv_sem=self.recv.at[self.count],
            device_id=tuple(peer),
            device_id_type=pl.DeviceIdType.MESH,
        )
        self.count += 1
        copy.start()
        self.all.append(copy)
        return copy


def kernel(order, sizes, p, x, out, reports, own, dev, rep, rep_recv, send_sem, recv_sem, own_sem, *bufs):
    groups, shares = PLANS[order]
    me = [lax.axis_index(name) for name in AXES]
    parts = chunks_of(p, shares)
    recvs = bufs[: len(groups)]
    curs = (own,) + bufs[len(groups) :]
    stages = gather_stages(sizes)
    rep_groups = ((0,), (1, 2))

    def peer_at(d):
        return [lax.rem(me[a] + d[a], sizes[a]) if d[a] else me[a] for a in range(3)]

    barrier = pltpu.get_barrier_semaphore()
    near = [set(group) for group in groups] + [set(group) for group in rep_groups]
    near += [{axis for axis, _ in stage} for stage in stages]
    greeted = [d for d in offsets_of((0, 1, 2), sizes) if any({a for a in range(3) if d[a]} <= axes for axes in near)]
    for d in greeted:
        pl.semaphore_signal(barrier, inc=1, device_id=tuple(peer_at(d)), device_id_type=pl.DeviceIdType.MESH)

    owns = []
    for k, (lo, size) in enumerate(parts):
        index = [me[a] if a in groups[0] else slice(None) for a in range(3)]
        rest = (slice(None),) * (3 - len(groups[0]))
        copy = pltpu.make_async_copy(x.at[(*index, pl.ds(lo, size))], own.at[(*rest, pl.ds(lo, size))], own_sem.at[k])
        copy.start()
        owns.append(copy)
    dev[...] = jnp.zeros_like(dev)
    pl.semaphore_wait(barrier, len(greeted))

    copies = Copies(send_sem, recv_sem)
    waiting = {}

    def left_at(g):
        return sorted(a for group in groups[g:] for a in group)

    def scatter(g, k):
        span = pl.ds(*parts[k])
        source = x if g == 0 else curs[g]
        left, rest = left_at(g), left_at(g + 1)
        waiting[g, k] = []
        for slot, d in enumerate(offsets_of(groups[g], sizes)):
            peer = peer_at(d)
            index = tuple(peer[a] if a in groups[g] else slice(None) for a in left)
            place = recvs[g].at[(slot, *[slice(None)] * len(rest), span)]
            waiting[g, k].append(copies.start(source.at[(*index, span)], place, peer))

    def settle(g, k):
        for copy in waiting[g, k]:
            copy.wait_recv()
        if g == 0:
            owns[k].wait()
        lo, size = parts[k]
        left, rest = left_at(g), left_at(g + 1)
        first = sum(len(group) for group in groups[:g])
        worst = {}
        for place in itertools.product(*[range(sizes[a]) for a in rest]):
            for t in range(lo, lo + size):
                where = dict(zip(rest, place))
                if g == 0:
                    mine = own[(*place, t)]
                else:
                    mine = curs[g][(*[where.get(a, me[a]) for a in left], t)]
                values = {(0, 0, 0): mine}
                for slot, d in enumerate(offsets_of(groups[g], sizes)):
                    values[d] = recvs[g][(slot, *place, t)]
                for r, axis in enumerate(groups[g], first):
                    members = {}
                    for d, value in values.items():
                        members.setdefault((*d[:axis], 0, *d[axis + 1 :]), []).append(value)
                    values = {}
                    for d, group in members.items():
                        mean = mean_of(functools.reduce(jnp.add, group), len(group))
                        values[d] = mean
                        for value in group:
                            gap = jnp.abs(value - mean)
                            worst[r] = jnp.maximum(worst[r], gap) if r in worst else gap
                (mean,) = values.values()
                if g == len(groups) - 1:
                    out[(me[0], me[1], me[2], t)] = mean
                else:
                    curs[g + 1][(*place, t)] = mean
        for r, gap in worst.items():
            dev[r] = jnp.maximum(dev[r], gap)

    held = {}

    def gather(k, s):
        span = pl.ds(*parts[k])
        if s == 0:
            held[k] = [[me[0]], [me[1]], [me[2]]]
        have = held[k]
        blocks = list(itertools.product(*[[slice(None)] if h is None else h for h in have]))
        choices = []
        for axis, bit in stages[s]:
            if bit is None:
                n = sizes[axis]
                choices.append([(axis, me[axis])] + [(axis, lax.rem(me[axis] + d, n)) for d in range(1, n)])
            else:
                choices.append([(axis, bit, 0), (axis, bit, 1)])
        waiting["gather", k] = []
        for number, choice in enumerate(itertools.product(*choices)):
            if number == 0:
                continue
            peer = list(me)
            flips = 0
            for part in choice:
                if len(part) == 2:
                    peer[part[0]] = part[1]
                elif part[2]:
                    high = lax.rem(me[part[0]] // part[1], 2)
                    flips = flips + part[1] - 2 * part[1] * high
                    peer[part[0]] = me[part[0]] + flips
            for block in blocks:
                piece = out.at[(*block, span)]
                waiting["gather", k].append(copies.start(piece, piece, peer))
        for axis, bit in stages[s]:
            if bit is None or bit == 1:
                have[axis] = None
            else:
                turn = bit - 2 * bit * lax.rem(me[axis] // bit, 2)
                have[axis] = have[axis] + [i + turn for i in have[axis]]

    def landed(k):
        for copy in waiting["gather", k]:
            copy.wait_recv()

    def tell(s):
        base = sum(len(offsets_of(group, sizes)) for group in rep_groups[:s])
        if s == 0:
            rows = lax.broadcasted_iota(jnp.int32, (SUBLANES, LANES), 0)
            tile = jnp.zeros((SUBLANES, LANES), jnp.float32)
            for r in range(3):
                tile = jnp.where(rows == r, jnp.max(dev[r]), tile)
            rep[0] = tile
        waiting["rep", s] = []
        for slot, d in enumerate(offsets_of(rep_groups[s], sizes), base):
            waiting["rep", s].append(copies.start(rep.at[s], rep_recv.at[slot], peer_at(d)))

    def told(s):
        base = sum(len(offsets_of(group, sizes)) for group in rep_groups[:s])
        for copy in waiting["rep", s]:
            copy.wait_recv()
        tile = rep[s]
        for slot in range(base, base + len(waiting["rep", s])):
            tile = jnp.maximum(tile, rep_recv[slot])
        if s == 0:
            rep[1] = tile
        else:
            for r in range(3):
                reports[r] = jnp.max(tile[r : r + 1])

    for k in range(len(parts)):
        scatter(0, k)

    events = []
    whole = FIRST_US[order[0]]
    for k, (lo, size) in enumerate(parts):
        at = whole * (lo + size) / p

        def reduce_step(g, k):
            settle(g, k)
            if g + 1 < len(groups):
                scatter(g + 1, k)
            else:
                gather(k, 0)

        for g in range(len(groups)):
            events.append((at + g * STEP_US, k, functools.partial(reduce_step, g, k)))
        if order[0] == 0:
            at = whole
        at += (len(groups) - 1) * STEP_US

        def gather_step(k, s):
            landed(k)
            if s < len(stages):
                gather(k, s)

        for s in range(1, len(stages) + 1):
            events.append((at + s * STEP_US, k, functools.partial(gather_step, k, s)))
        if k == len(parts) - 1:

            def rep_step(s):
                if s:
                    told(s - 1)
                if s < 2:
                    tell(s)

            for s in range(3):
                events.append((at + s * STEP_US + 0.1, k, functools.partial(rep_step, s)))
    for _, _, step in sorted(events, key=lambda event: event[:2]):
        step()
    for copy in copies.all:
        copy.wait_send()


def run(which, order, sizes, p, x):
    tile = (SUBLANES, LANES)
    f32 = jnp.float32
    groups, shares = PLANS[order]
    parts = len(chunks_of(p, shares))
    reps = len(offsets_of((0,), sizes)) + len(offsets_of((1, 2), sizes))
    copies = reps + parts * sum(len(offsets_of(group, sizes)) for group in groups)
    copies += parts * gather_count(sizes)
    recvs, curs = [], []
    for g, group in enumerate(groups):
        rest = [sizes[a] for a in sorted(a for later in groups[g + 1 :] for a in later)]
        recvs.append(pltpu.VMEM((len(offsets_of(group, sizes)), *rest, p, *tile), f32))
        if g == 0:
            own = pltpu.VMEM((*rest, p, *tile), f32)
        if g + 1 < len(groups):
            curs.append(pltpu.VMEM((*rest, p, *tile), f32))
    scratch = [own, pltpu.VMEM((3, *tile), f32), pltpu.VMEM((2, *tile), f32), pltpu.VMEM((reps, *tile), f32)]
    scratch += [pltpu.SemaphoreType.DMA((copies,)), pltpu.SemaphoreType.DMA((copies,)), pltpu.SemaphoreType.DMA((parts,))]
    return pl.pallas_call(
        functools.partial(kernel, order, sizes, p),
        out_shape=(jax.ShapeDtypeStruct(x.shape, f32), jax.ShapeDtypeStruct((3,), f32)),
        in_specs=[pl.BlockSpec(memory_space=pl.ANY)],
        out_specs=(pl.BlockSpec(memory_space=pltpu.VMEM), pl.BlockSpec(memory_space=pltpu.SMEM)),
        scratch_shapes=scratch + recvs + curs,
        compiler_params=pltpu.CompilerParams(collective_id=which, has_side_effects=True),
        name=f"moshpit_{which}",
    )(x)


def on_device(sizes, grads, plan):
    rows, columns = grads.shape[-2:]
    high, wide = rows // SUBLANES, columns // LANES
    tiles = high * wide
    p = -(-tiles // math.prod(sizes))
    x = grads.reshape(high, SUBLANES, wide, LANES).transpose(0, 2, 1, 3).reshape(tiles, SUBLANES, LANES)
    spare = p * math.prod(sizes) - tiles
    if spare:
        x = jnp.pad(x, ((0, spare), (0, 0), (0, 0)))
    x = x.reshape(*sizes, p, SUBLANES, LANES)
    orders = [(0, 1, 2), (0, 2, 1), (1, 0, 2), (1, 2, 0), (1, 2, 0), (2, 0, 1), (2, 1, 0)]
    names = {order: i for i, order in enumerate(PLANS)}
    branches = [functools.partial(run, names[order], order, sizes, p) for order in orders]
    place = lax.iota(jnp.int32, 3)
    choice = jnp.sum(plan * ((3 - place) * (2 - place) // 2)) - 1
    out, reports = lax.switch(choice, branches, x)
    out = out.reshape(-1, SUBLANES, LANES)[:tiles]
    out = out.reshape(high, wide, SUBLANES, LANES).transpose(0, 2, 1, 3).reshape(grads.shape)
    return out, reports


def solution(mesh):
    sizes = tuple(mesh.shape[name] for name in AXES)
    placed = (P("gx", "gy", "gz", None, None), P())
    return jax.shard_map(
        functools.partial(on_device, sizes), mesh=mesh, in_specs=placed, out_specs=placed, check_vma=False
    )
```
